32 devices in a mesh: dp: 4 (over y, x), seq: 8 (over z, core).
Axes of the slice: x: 2, y: 2, z: 4, core: 2. Of those that a mesh axis runs over, the one named last changes fastest.
Arguments:
- projected: bfloat16 [4, 1024, 6144], P('dp', 'seq'), may hold values from -24 to 24
- upstream: bfloat16 [4, 1024, 2048], P('dp', 'seq'), may hold values from -6 to 6
- w_out: bfloat16 [2048, 2048], replicated, may hold values from -0.125 to 0.125
- partners: int32 [8, 3], replicated, may hold values from 0 to 7, as said below
Outputs:
- grad_projected: bfloat16 [4, 1024, 6144], P('dp', 'seq')
- grad_w_out: float32 [2048, 2048], P(None, ('dp', 'seq'))
The draws below stay inside these ranges and needn't reach their ends.
Inputs may be any that keep to these rules, and one draw needn't show every extreme that they name: `partners`: split the 8 blocks into runs of 1 block; column r maps each run one to one onto the run that lies (r + 1) * 1 runs later, counted cyclically.
All inputs are finite; a program needn't handle non-finite values.
Results may differ from the reference program's by a relative error of at most 0.0064.
Values may be sent and summed in bfloat16 or wider, within the bound.
A program may use at most 192 MiB of HBM per device.

```python
from functools import partial
import jax
import jax.numpy as jnp
from jax import lax

D = 2048
HD = 128
HW = 16
BLOCK = 128
RAND = 3
TOK_DEV = 128
LEN = 1024
SEQS = 4
NB = 8


def draw_projected(key, part):
    first = jax.random.fold_in(key, 0)
    width = HW * HD
    shape = (SEQS, LEN, 3 * width)
    base = jnp.clip(jax.random.normal(first, shape, jnp.float32), -4.0, 4.0)
    return base.astype(jnp.bfloat16)


def shuffled(single, count):
    return jax.random.permutation(single, count)


def draw_partners(key, part):
    per_run = TOK_DEV // BLOCK
    runs = NB // per_run
    spacing = runs // (2 * RAND + 1)
    many_keys = jax.random.split(key, RAND * runs)
    orders = jax.vmap(partial(shuffled, count=per_run))(many_keys).astype(jnp.int32).reshape(RAND, runs, per_run)
    run_ids = jnp.arange(runs, dtype=jnp.int32)
    columns = []
    for step in range(RAND):
        target = (run_ids + (step + 1) * spacing) % runs
        columns.append((target[:, None] * per_run + orders[step]).reshape(NB))
    return jnp.stack(columns, axis=1).astype(jnp.int32)


def raised(values, rng, source, target, parts, factor):
    def block_of(position):
        return (jnp.arange(values.shape[position]) // (values.shape[position] // parts)).reshape((-1,) + (1,) * (values.ndim - 1 - position))

    one_side = jax.random.permutation(rng, parts)[block_of(target)]
    other_side = (block_of(target) + parts // 2) % parts
    return jnp.where((block_of(source) == one_side) | (block_of(source) == other_side), factor * values, values)


def level_of(own_key, shape, pieces, smallest, largest):
    factor_of = 1.0
    for dim, parts in pieces:
        draws = jax.random.uniform(jax.random.fold_in(jax.random.fold_in(own_key, 6), dim), (parts,), jnp.float32, smallest / len(pieces), largest / len(pieces))
        factor_of = factor_of * jnp.repeat(jnp.exp(draws), shape[dim] // parts).reshape((-1,) + (1,) * (len(shape) - 1 - dim))
    return factor_of


def scatter_about(rng, extent, deviation, bound, shards=(), held_as=jnp.bfloat16):
    result = jax.random.normal(rng, extent, jnp.float32) * deviation
    if len(shards) > 0:
        result = level_of(rng, extent, shards, -0.22, 0.18) * result
    return jnp.clip(result, min=-bound, max=bound).astype(held_as)


def heavy_noise(rng, shape, deviation, reach, shards, heavy, kind=jnp.bfloat16):
    result = deviation * jax.random.normal(rng, shape, jnp.float32)
    if shards:
        result = result * level_of(rng, shape, shards, -0.22, 0.18)
    return jnp.clip(raised(result, jax.random.fold_in(rng, 3), *heavy), -reach, reach).astype(kind)


def setup_inputs(seed: int = 0) -> dict:
    arg_keys = jax.random.split(jax.random.key(seed), 5)
    return {
        "projected": draw_projected(jax.random.fold_in(arg_keys[4], 71), 0),
        "upstream": heavy_noise(arg_keys[1], (SEQS, LEN, D), 1.0, 6.0, ((0, 4), (1, 8)), (1, 2, 8, 2.0)),
        "w_out": scatter_about(arg_keys[2], (HW * HD, D), (HW * HD) ** -0.5, 0.125),
        "partners": draw_partners(jax.random.fold_in(arg_keys[4], 71), 0),
    }


def round_half(value):
    return lax.optimization_barrier(value.astype(jnp.bfloat16)).astype(jnp.float32)


def block_links(partners):
    block_ids = jnp.arange(NB, dtype=jnp.int32)
    chosen = jnp.any(partners[:, :, None] == block_ids[None, None, :], axis=1)
    nearby = jnp.abs(block_ids[:, None] - block_ids[None, :]) <= 1
    border = (block_ids == 0) | (block_ids == NB - 1)
    return chosen | chosen.T | nearby | border[:, None] | border[None, :]


def one_sequence(projected, upstream, w_out, links):
    width = HW * HD
    scale = HD ** -0.5
    queries = projected[:, :width].astype(jnp.float32).reshape(LEN, HW, HD)
    keys = projected[:, width:2 * width].astype(jnp.float32).reshape(LEN, HW, HD)
    values = projected[:, 2 * width:].astype(jnp.float32).reshape(LEN, HW, HD)
    out_grad_all = jnp.dot(upstream, w_out.T, preferred_element_type=jnp.float32).astype(jnp.bfloat16)

    def block_step(carry, index):
        start = (index * BLOCK).astype(jnp.int32)
        query = lax.dynamic_slice_in_dim(queries, start, BLOCK, 0)
        out_grad = lax.dynamic_slice_in_dim(out_grad_all, start, BLOCK, 0).astype(jnp.float32).reshape(BLOCK, HW, HD)
        link_row = lax.dynamic_index_in_dim(links, index.astype(jnp.int32), 0, keepdims=False)
        visible = jnp.repeat(link_row, BLOCK)[None, None, :]
        scores = jnp.einsum("qhd,khd->hqk", query, keys) * scale
        scores = jnp.where(visible, scores, -1e30)
        row_max = jnp.max(scores, axis=2, keepdims=True)
        exponent = jnp.where(visible, jnp.exp(scores - row_max), 0.0)
        total = jnp.sum(exponent, axis=2, keepdims=True)
        attended = jnp.einsum("hqk,khd->hqd", round_half(exponent), values) / total
        attended = jnp.transpose(attended, (1, 0, 2))
        probs = exponent / total
        prob_grad = jnp.einsum("qhd,khd->hqk", out_grad, values)
        delta = jnp.transpose(jnp.sum(out_grad * attended, axis=2), (1, 0))[:, :, None]
        score_grad = round_half(probs * (prob_grad - delta))
        query_grad = jnp.einsum("hqk,khd->qhd", score_grad, keys) * scale
        key_term = jnp.einsum("hqk,qhd->khd", score_grad, query) * scale
        value_term = jnp.einsum("hqk,qhd->khd", round_half(probs), out_grad)
        partial_value = jnp.concatenate([key_term.reshape(LEN, width), value_term.reshape(LEN, width)], axis=1)
        return carry + round_half(partial_value), (query_grad.reshape(BLOCK, width), attended.reshape(BLOCK, width))

    start_carry = jnp.zeros((LEN, 2 * width), jnp.float32)
    key_grads, (query_grad, attended) = lax.scan(block_step, start_carry, jnp.arange(NB, dtype=jnp.int32))
    qkv_grad = jnp.concatenate([query_grad.reshape(LEN, width), key_grads], axis=1).astype(jnp.bfloat16)
    attended_out = attended.reshape(LEN, width).astype(jnp.bfloat16)
    grad_w_out = jnp.dot(attended_out.T, upstream, preferred_element_type=jnp.float32)
    return qkv_grad, grad_w_out


def reference(projected, upstream, w_out, partners):
    links = block_links(partners)

    def each(index):
        return one_sequence(projected[index], upstream[index], w_out, links)

    grad_projected, grad_w_out = lax.map(each, jnp.arange(SEQS, dtype=jnp.int32))
    factor = (SEQS * LEN) ** -0.5
    return grad_projected, jnp.sum(grad_w_out, axis=0) * factor
```

```python
import functools

import jax
import jax.numpy as jnp
from jax import lax
from jax.experimental import pallas as pl
from jax.experimental.pallas import tpu as pltpu
from jax.sharding import PartitionSpec as P

HD = 128
BLOCK = 128
MESH = pl.DeviceIdType.MESH
VMEM = pl.BlockSpec(memory_space=pltpu.VMEM)


def remote(src, dst, send_sem, recv_sem, **where):
    return pltpu.make_async_remote_copy(
        src_ref=src,
        dst_ref=dst,
        send_sem=send_sem,
        recv_sem=recv_sem,
        device_id=where,
        device_id_type=MESH,
    )


def greet(axes):
    barrier = pltpu.get_barrier_semaphore()
    count = 0
    for axis, size in axes:
        me = lax.axis_index(axis)
        for k in range(1, size):
            pl.semaphore_signal(
                barrier, inc=1, device_id={axis: lax.rem(me + k, size)}, device_id_type=MESH
            )
            count += 1
    pl.semaphore_wait(barrier, count)


def gather_kernel(
    n, proj_ref, up_ref, qkv_ref, u_ref, send, recv, r_send, r_recv, l_send, l_recv, p_send, p_recv,
    own_sem,
):
    me = lax.axis_index("seq")
    rows = proj_ref.shape[0]
    width = proj_ref.shape[1] // 3
    w = width // n
    chips = n // 2
    z = me // 2
    core = lax.rem(me, 2)
    partner = me + 1 - 2 * core

    def u_rows(index):
        return u_ref.at[pl.ds(pl.multiple_of(index * rows, rows), rows), :]

    def right(k, src):
        return remote(src, u_rows(me - 2 * k), r_send.at[k], r_recv.at[k], seq=me + 2)

    def left(k, src):
        return remote(src, u_rows(me + 2 * k), l_send.at[k], l_recv.at[k], seq=me - 2)

    def across(index, src):
        return remote(src, u_rows(index), p_send.at[index // 2], p_recv.at[index // 2], seq=partner)

    greet((("seq", n),))
    copies = []
    for k in range(1, n):
        p = lax.rem(me + k, n)
        for t in range(3):
            copy = remote(
                proj_ref.at[:, pl.ds(pl.multiple_of(t * width + p * w, w), w)],
                qkv_ref.at[t, pl.ds(pl.multiple_of(me * rows, rows), rows), :],
                send.at[t, k],
                recv.at[t, k],
                seq=p,
            )
            copy.start()
            copies.append(copy)

    @pl.when(z + 1 < chips)
    def _():
        right(0, up_ref).start()

    @pl.when(z >= 1)
    def _():
        left(0, up_ref).start()

    across(me, up_ref).start()
    owns = [
        pltpu.make_async_copy(
            proj_ref.at[:, pl.ds(pl.multiple_of(t * width + me * w, w), w)],
            qkv_ref.at[t, pl.ds(pl.multiple_of(me * rows, rows), rows), :],
            own_sem.at[t],
        )
        for t in range(3)
    ]
    owns.append(pltpu.make_async_copy(up_ref, u_rows(me), own_sem.at[3]))
    for copy in owns:
        copy.start()
    for k in range(1, chips):

        @pl.when(z - k >= 0)
        def _():
            right(k - 1, up_ref).wait_recv()
            block = me - 2 * k
            across(block, u_rows(block)).start()

            @pl.when(z + 1 < chips)
            def _():
                right(k, u_rows(block)).start()

        @pl.when(z + k < chips)
        def _():
            left(k - 1, up_ref).wait_recv()
            block = me + 2 * k
            across(block, u_rows(block)).start()

            @pl.when(z >= 1)
            def _():
                left(k, u_rows(block)).start()

    for copy in owns:
        copy.wait()
    for copy in copies:
        copy.wait()
    for i in range(chips):
        across(2 * i + core, up_ref).wait()
    for k in range(chips):

        @pl.when((z - k >= 0) & (z + 1 < chips))
        def _():
            right(k, up_ref).wait_send()

        @pl.when((z + k < chips) & (z >= 1))
        def _():
            left(k, up_ref).wait_send()


def gather(n, proj, up):
    rows, width3 = proj.shape
    w = width3 // 3 // n
    chips = n // 2
    dma = pltpu.SemaphoreType.DMA
    return pl.pallas_call(
        functools.partial(gather_kernel, n),
        out_shape=(
            jax.ShapeDtypeStruct((3, n * rows, w), proj.dtype),
            jax.ShapeDtypeStruct((n * rows, up.shape[1]), up.dtype),
        ),
        in_specs=[VMEM] * 2,
        out_specs=(VMEM, VMEM),
        scratch_shapes=[dma((3, n)), dma((3, n))] + [dma((chips,))] * 6 + [dma((4,))],
        compiler_params=pltpu.CompilerParams(collective_id=0, has_side_effects=True),
        name="gather",
    )(proj, up)


def attention_kernel(
    factor, q_ref, k_ref, v_ref, u_ref, w_ref, bias_ref, dq_ref, dk_ref, dv_ref, dw_ref,
    dk_acc, dv_acc, dw_acc,
):
    step = pl.program_id(1)
    scale = HD ** (-0.5)
    q, k, v = q_ref[0], k_ref[0], v_ref[0]
    length, tile = k.shape[0], q.shape[0]
    f32, bf16 = jnp.float32, jnp.bfloat16

    def dot(a, b, da, db):
        return lax.dot_general(a, b, (((da,), (db,)), ((), ())), preferred_element_type=f32)

    u = u_ref[pl.ds(pl.multiple_of(step * tile, tile), tile), :]
    grad_t = dot(w_ref[...], u, 1, 1).astype(bf16)
    grad_t32 = grad_t.astype(f32)
    grad = grad_t32.T.astype(bf16)
    blocks = bias_ref.shape[1]
    scores = dot(k, q, 1, 1) * scale
    scores = (scores.reshape(blocks, BLOCK, tile) + bias_ref[0][:, None, :]).reshape(length, tile)
    exponent = jnp.exp(scores - jnp.max(scores, axis=0, keepdims=True))
    inverse = 1.0 / jnp.sum(exponent, axis=0, keepdims=True)
    att = dot(v, exponent.astype(bf16), 0, 0) * inverse
    delta = jnp.sum(grad_t32 * att, axis=0, keepdims=True)
    probs = exponent * inverse
    score_grad = (probs * (dot(v, grad_t, 1, 0) - delta)).astype(bf16)
    dq_ref[...] = (dot(k, score_grad, 0, 0) * scale).T.astype(bf16)
    dk = dot(score_grad, q, 1, 0)
    dv = dot(probs.astype(bf16), grad, 1, 0)
    dw = dot(att.astype(bf16), u, 1, 0)

    @pl.when(step == 0)
    def _():
        dk_acc[...] = dk
        dv_acc[...] = dv
        dw_acc[...] = dw

    @pl.when(step > 0)
    def _():
        dk_acc[...] += dk
        dv_acc[...] += dv
        dw_acc[...] += dw

    @pl.when(step == pl.num_programs(1) - 1)
    def _():
        dk_ref[...] = (dk_acc[...] * scale).astype(bf16)
        dv_ref[...] = dv_acc[...].astype(bf16)
        dw_ref[...] = (dw_acc[...] * factor).astype(bf16)


def attention(factor, qkv, u_all, w_mine, bias):
    length, w = qkv.shape[1:]
    columns = u_all.shape[1]
    tile = min(2 * BLOCK, length)
    blocks = length // BLOCK
    bf16 = jnp.bfloat16
    bias_tiles = bias.reshape(blocks, length // tile, tile).transpose(1, 0, 2)
    return pl.pallas_call(
        functools.partial(attention_kernel, factor),
        grid=(w // HD, length // tile),
        out_shape=[jax.ShapeDtypeStruct((length, w), bf16)] * 3
        + [jax.ShapeDtypeStruct((w, columns), bf16)],
        in_specs=[
            pl.BlockSpec((1, tile, HD), lambda h, i: (0, i, h)),
            pl.BlockSpec((1, length, HD), lambda h, i: (1, 0, h)),
            pl.BlockSpec((1, length, HD), lambda h, i: (2, 0, h)),
            pl.BlockSpec((length, columns), lambda h, i: (0, 0)),
            pl.BlockSpec((HD, columns), lambda h, i: (h, 0)),
            pl.BlockSpec((1, blocks, tile), lambda h, i: (i, 0, 0)),
        ],
        out_specs=[
            pl.BlockSpec((tile, HD), lambda h, i: (i, h)),
            pl.BlockSpec((length, HD), lambda h, i: (0, h)),
            pl.BlockSpec((length, HD), lambda h, i: (0, h)),
            pl.BlockSpec((HD, columns), lambda h, i: (h, 0)),
        ],
        scratch_shapes=[
            pltpu.VMEM((length, HD), jnp.float32),
            pltpu.VMEM((length, HD), jnp.float32),
            pltpu.VMEM((HD, columns), jnp.float32),
        ],
        compiler_params=pltpu.CompilerParams(dimension_semantics=("arbitrary", "arbitrary")),
        name="attention",
    )(qkv, qkv, qkv, u_all, w_mine, bias_tiles)


def return_kernel(
    n, groups, dq_ref, dk_ref, dv_ref, dw_ref, grad_ref, out_ref, held, total, d_send, d_recv,
    send, recv, w_send, w_recv, own_sem,
):
    me, mine = lax.axis_index("seq"), lax.axis_index("dp")
    length, w = dq_ref.shape
    rows = length // n
    part = dw_ref.shape[1] // groups
    columns = part // n
    greet((("seq", n), ("dp", groups)))
    sums = []
    for k in range(1, groups):
        p = lax.rem(mine + k, groups)
        copy = remote(
            dw_ref.at[:, pl.ds(pl.multiple_of(p * part, part), part)],
            held.at[k - 1],
            d_send.at[k],
            d_recv.at[k],
            dp=p,
        )
        copy.start()
        sums.append(copy)
    copies = []
    place = [
        pl.ds(pl.multiple_of(t * n * w + me * w, w), w) for t in range(3)
    ]
    for k in range(1, n):
        p = lax.rem(me + k, n)
        for t, ref in enumerate((dq_ref, dk_ref, dv_ref)):
            copy = remote(
                ref.at[pl.ds(pl.multiple_of(p * rows, rows), rows), :],
                grad_ref.at[:, place[t]],
                send.at[t, k],
                recv.at[t, k],
                seq=p,
            )
            copy.start()
            copies.append(copy)
    owns = [
        pltpu.make_async_copy(
            ref.at[pl.ds(pl.multiple_of(me * rows, rows), rows), :],
            grad_ref.at[:, place[t]],
            own_sem.at[t],
        )
        for t, ref in enumerate((dq_ref, dk_ref, dv_ref))
    ]
    for copy in owns:
        copy.start()
    for copy in sums:
        copy.wait()
    summed = dw_ref[:, pl.ds(pl.multiple_of(mine * part, part), part)].astype(jnp.float32)
    for k in range(groups - 1):
        summed = summed + held[k].astype(jnp.float32)
    total[...] = summed.T.astype(total.dtype)

    def columns_of(p):
        return total.at[pl.ds(pl.multiple_of(p * columns, columns), columns), :]

    spot = out_ref.at[:, pl.ds(pl.multiple_of(me * w, w), w)]
    for k in range(1, n):
        p = lax.rem(me + k, n)
        copy = remote(columns_of(p), spot, w_send.at[k], w_recv.at[k], seq=p)
        copy.start()
        copies.append(copy)
    own = pltpu.make_async_copy(columns_of(me), spot, own_sem.at[3])
    own.start()
    for copy in owns + [own] + copies:
        copy.wait()


def give_back(n, groups, dq, dk, dv, dw):
    length, w = dq.shape
    part = dw.shape[1] // groups
    dma = pltpu.SemaphoreType.DMA
    return pl.pallas_call(
        functools.partial(return_kernel, n, groups),
        out_shape=(
            jax.ShapeDtypeStruct((length // n, 3 * n * w), dq.dtype),
            jax.ShapeDtypeStruct((part // n, n * w), dw.dtype),
        ),
        in_specs=[VMEM] * 4,
        out_specs=(VMEM, VMEM),
        scratch_shapes=[
            pltpu.VMEM((max(groups - 1, 1), w, part), dw.dtype),
            pltpu.VMEM((part, w), dw.dtype),
            dma((groups,)),
            dma((groups,)),
            dma((3, n)),
            dma((3, n)),
            dma((n,)),
            dma((n,)),
            dma((4,)),
        ],
        compiler_params=pltpu.CompilerParams(collective_id=1, has_side_effects=True),
        name="give_back",
    )(dq, dk, dv, dw)


def block_bias(partners, total):
    ids = jnp.arange(total, dtype=jnp.int32)
    chosen = jnp.any(partners[:, :, None] == ids[None, None, :], axis=1)
    near = jnp.abs(ids[:, None] - ids[None, :]) <= 1
    border = (ids == 0) | (ids == total - 1)
    linked = chosen | chosen.T | near | border[:, None] | border[None, :]
    return jnp.repeat(jnp.where(linked, 0.0, -1e30).astype(jnp.float32), BLOCK, axis=1)


def on_device(projected, upstream, w_out, partners):
    n, groups = lax.axis_size("seq"), lax.axis_size("dp")
    rows = projected.shape[1]
    w = w_out.shape[0] // n
    factor = (rows * n * groups) ** (-0.5)
    qkv, u_all = gather(n, projected[0], upstream[0])
    w_mine = lax.dynamic_slice_in_dim(w_out, lax.axis_index("seq") * w, w, 0)
    bias = block_bias(partners, rows * n // BLOCK)
    dq, dk, dv, dw = attention(factor, qkv, u_all, w_mine, bias)
    grad, dw_t = give_back(n, groups, dq, dk, dv, dw)
    return grad[None], dw_t.T.astype(jnp.float32)


def solution(mesh):
    return jax.shard_map(
        on_device,
        mesh=mesh,
        in_specs=(P("dp", "seq", None), P("dp", "seq", None), P(), P()),
        out_specs=(P("dp", "seq", None), P(None, ("dp", "seq"))),
        check_vma=False,
    )
```

```python
import functools

import jax
import jax.numpy as jnp
from jax import lax
from jax.experimental import pallas as pl
from jax.experimental.pallas import tpu as pltpu
from jax.sharding import PartitionSpec as P

HD = 128
BLOCK = 128
MESH = pl.DeviceIdType.MESH
VMEM = pl.BlockSpec(memory_space=pltpu.VMEM)


def remote(src, dst, send_sem, recv_sem, **where):
    return pltpu.make_async_remote_copy(
        src_ref=src,
        dst_ref=dst,
        send_sem=send_sem,
        recv_sem=recv_sem,
        device_id=where,
        device_id_type=MESH,
    )


def greet(axes):
    barrier = pltpu.get_barrier_semaphore()
    count = 0
    for axis, size in axes:
        me = lax.axis_index(axis)
        for k in range(1, size):
            pl.semaphore_signal(
                barrier, inc=1, device_id={axis: lax.rem(me + k, size)}, device_id_type=MESH
            )
            count += 1
    pl.semaphore_wait(barrier, count)


def layer_kernel(
    n, groups, factor, proj_ref, up_ref, bias_ref, w_ref, grad_ref, out_ref, qkv, u_all, w_mine,
    og, kt, vt, dk_acc, dv_acc, dw_acc, grads, terms, held, total, q_send, q_recv, r_send, r_recv,
    l_send, l_recv, p_send, p_recv, g_send, g_recv, d_send, d_recv, w_send, w_recv, own_sem,
    own_q, own_g, own_w,
):
    me, mine = lax.axis_index("seq"), lax.axis_index("dp")
    rows = proj_ref.shape[0]
    width = proj_ref.shape[1] // 3
    length = n * rows
    heads = width // HD // n
    part = up_ref.shape[1] // groups
    columns = part // n
    chips = n // 2
    z = me // 2
    core = lax.rem(me, 2)
    partner = me + 1 - 2 * core
    scale = HD ** (-0.5)
    f32, bf16 = jnp.float32, jnp.bfloat16
    tile = min(2 * BLOCK, length)

    def dot(a, b, da, db):
        return lax.dot_general(a, b, (((da,), (db,)), ((), ())), preferred_element_type=f32)

    def span(index, size):
        return pl.ds(pl.multiple_of(index * size, size), size)

    def u_rows(index):
        return u_all.at[span(index, rows), :]

    def right(k, src):
        return remote(src, u_rows(me - 2 * k), r_send.at[k], r_recv.at[k], seq=me + 2)

    def left(k, src):
        return remote(src, u_rows(me + 2 * k), l_send.at[k], l_recv.at[k], seq=me - 2)

    def across(index, src):
        return remote(src, u_rows(index), p_send.at[index // 2], p_recv.at[index // 2], seq=partner)

    def head_columns(t, device, h):
        return span(t * n * heads + device * heads + h, HD)

    def send_head(h):
        started = []
        for k in range(1, n):
            p = lax.rem(me + k, n)
            for t in range(3):
                copy = remote(
                    proj_ref.at[:, head_columns(t, p, h)],
                    qkv.at[h, t, span(me, rows), :],
                    q_send.at[h, t, k],
                    q_recv.at[h, t, k],
                    seq=p,
                )
                copy.start()
                started.append(copy)
        for t in range(3):
            copy = pltpu.make_async_copy(
                proj_ref.at[:, head_columns(t, me, h)],
                qkv.at[h, t, span(me, rows), :],
                own_q.at[h, t],
            )
            copy.start()
            started.append(copy)
        return started

    load_w = pltpu.make_async_copy(w_ref.at[span(me, heads * HD), :], w_mine, own_sem.at[0])
    load_w.start()
    greet((("seq", n), ("dp", groups)))

    @pl.when(z + 1 < chips)
    def _():
        right(0, up_ref).start()

    @pl.when(z >= 1)
    def _():
        left(0, up_ref).start()

    across(me, up_ref).start()
    own_u = pltpu.make_async_copy(up_ref, u_rows(me), own_sem.at[1])
    own_u.start()
    arriving = []
    for k in range(1, chips):

        @pl.when(z - k >= 0)
        def _():
            right(k - 1, up_ref).wait_recv()
            block = me - 2 * k

            @pl.when(z + 1 < chips)
            def _():
                right(k, u_rows(block)).start()

            across(block, u_rows(block)).start()

        @pl.when(z + k < chips)
        def _():
            left(k - 1, up_ref).wait_recv()
            block = me + 2 * k

            @pl.when(z >= 1)
            def _():
                left(k, u_rows(block)).start()

            across(block, u_rows(block)).start()

        if len(arriving) < heads:
            arriving.append(send_head(len(arriving)))
    while len(arriving) < heads:
        arriving.append(send_head(len(arriving)))
    load_w.wait()
    own_u.wait()
    for i in range(chips):
        across(2 * i + core, up_ref).wait_recv()

    def out_grad_step(i, carry):
        u = u_all[span(i, tile), :]
        og[:, span(i, tile)] = dot(w_mine[...], u, 1, 1).astype(bf16)
        return carry

    lax.fori_loop(0, length // tile, out_grad_step, 0)
    leaving = []
    sums = []
    for h in range(heads):
        for copy in arriving[h]:
            copy.wait()
        kt[...] = qkv[h, 1].astype(f32).T.astype(bf16)
        vt[...] = qkv[h, 2].astype(f32).T.astype(bf16)
        dk_acc[...] = jnp.zeros_like(dk_acc)
        dv_acc[...] = jnp.zeros_like(dv_acc)
        dw_acc[...] = jnp.zeros_like(dw_acc)

        def tile_step(i, carry):
            at = span(i, tile)
            q, k, v = qkv[h, 0, at, :], qkv[h, 1], qkv[h, 2]
            grad_t = og[h * HD : (h + 1) * HD, at]
            grad_t32 = grad_t.astype(f32)
            scores = dot(k, q, 1, 1) * scale
            scores = scores.reshape(length // BLOCK, BLOCK, tile) + bias_ref[:, at][:, None, :]
            scores = scores.reshape(length, tile)
            exponent = jnp.exp(scores - jnp.max(scores, axis=0, keepdims=True))
            inverse = 1.0 / jnp.sum(exponent, axis=0, keepdims=True)
            att = dot(vt[...], exponent.astype(bf16), 1, 0) * inverse
            delta = jnp.sum(grad_t32 * att, axis=0, keepdims=True)
            probs = exponent * inverse
            score_grad = (probs * (dot(v, grad_t, 1, 0) - delta)).astype(bf16)
            grads[h, 0, at, :] = (dot(kt[...], score_grad, 1, 0) * scale).T.astype(bf16)
            dk_acc[...] += dot(score_grad, q, 1, 0)
            dv_acc[...] += dot(probs.astype(bf16), grad_t32.T.astype(bf16), 1, 0)
            dw_acc[...] += dot(att.astype(bf16), u_all[at, :], 1, 0)
            return carry

        lax.fori_loop(0, length // tile, tile_step, 0)
        terms[h] = (dw_acc[...] * factor).astype(bf16)
        for k in range(1, groups):
            p = lax.rem(mine + k, groups)
            copy = remote(
                terms.at[h, :, span(p, part)],
                held.at[h, k - 1],
                d_send.at[h, k],
                d_recv.at[h, k],
                dp=p,
            )
            copy.start()
            sums.append(copy)
        grads[h, 1] = (dk_acc[...] * scale).astype(bf16)
        grads[h, 2] = dv_acc[...].astype(bf16)
        for k in range(1, n):
            p = lax.rem(me + k, n)
            for t in range(3):
                copy = remote(
                    grads.at[h, t, span(p, rows), :],
                    grad_ref.at[:, head_columns(t, me, h)],
                    g_send.at[h, t, k],
                    g_recv.at[h, t, k],
                    seq=p,
                )
                copy.start()
                leaving.append(copy)
        for t in range(3):
            copy = pltpu.make_async_copy(
                grads.at[h, t, span(me, rows), :],
                grad_ref.at[:, head_columns(t, me, h)],
                own_g.at[h, t],
            )
            copy.start()
            leaving.append(copy)
    for copy in sums:
        copy.wait()
    for h in range(heads):
        summed = terms[h, :, span(mine, part)].astype(f32)
        for k in range(groups - 1):
            summed = summed + held[h, k].astype(f32)
        total[h] = summed.T.astype(bf16)
        spot = out_ref.at[:, span(me * heads + h, HD)]
        for k in range(1, n):
            p = lax.rem(me + k, n)
            copy = remote(
                total.at[h, span(p, columns), :], spot, w_send.at[h, k], w_recv.at[h, k], seq=p
            )
            copy.start()
            leaving.append(copy)
        copy = pltpu.make_async_copy(total.at[h, span(me, columns), :], spot, own_w.at[h])
        copy.start()
        leaving.append(copy)
    for copy in leaving:
        copy.wait()
    for i in range(chips):
        across(2 * i + core, up_ref).wait_send()
    for k in range(chips):

        @pl.when((z - k >= 0) & (z + 1 < chips))
        def _():
            right(k, up_ref).wait_send()

        @pl.when((z + k < chips) & (z >= 1))
        def _():
            left(k, up_ref).wait_send()


def layer(n, groups, factor, proj, up, bias, w_out):
    rows, width3 = proj.shape
    width = width3 // 3
    heads = width // HD // n
    length, depth = n * rows, up.shape[1]
    part = depth // groups
    chips = n // 2
    f32, bf16 = jnp.float32, jnp.bfloat16
    dma = pltpu.SemaphoreType.DMA
    return pl.pallas_call(
        functools.partial(layer_kernel, n, groups, factor),
        out_shape=(
            jax.ShapeDtypeStruct((rows, width3), bf16),
            jax.ShapeDtypeStruct((part // n, width), bf16),
        ),
        in_specs=[VMEM] * 3 + [pl.BlockSpec(memory_space=pl.ANY)],
        out_specs=(VMEM, VMEM),
        scratch_shapes=[
            pltpu.VMEM((heads, 3, length, HD), bf16),
            pltpu.VMEM((length, depth), bf16),
            pltpu.VMEM((heads * HD, depth), bf16),
            pltpu.VMEM((heads * HD, length), bf16),
            pltpu.VMEM((HD, length), bf16),
            pltpu.VMEM((HD, length), bf16),
            pltpu.VMEM((length, HD), f32),
            pltpu.VMEM((length, HD), f32),
            pltpu.VMEM((HD, depth), f32),
            pltpu.VMEM((heads, 3, length, HD), bf16),
            pltpu.VMEM((heads, HD, depth), bf16),
            pltpu.VMEM((heads, max(groups - 1, 1), HD, part), bf16),
            pltpu.VMEM((heads, part, HD), bf16),
            dma((heads, 3, n)),
            dma((heads, 3, n)),
        ]
        + [dma((chips,))] * 6
        + [
            dma((heads, 3, n)),
            dma((heads, 3, n)),
            dma((heads, groups)),
            dma((heads, groups)),
            dma((heads, n)),
            dma((heads, n)),
            dma((2,)),
            dma((heads, 3)),
            dma((heads, 3)),
            dma((heads,)),
        ],
        compiler_params=pltpu.CompilerParams(
            collective_id=0, has_side_effects=True, vmem_limit_bytes=60 * 2**20
        ),
        name="layer",
    )(proj, up, bias, w_out)


def block_bias(partners, total):
    ids = jnp.arange(total, dtype=jnp.int32)
    chosen = jnp.any(partners[:, :, None] == ids[None, None, :], axis=1)
    near = jnp.abs(ids[:, None] - ids[None, :]) <= 1
    border = (ids == 0) | (ids == total - 1)
    linked = chosen | chosen.T | near | border[:, None] | border[None, :]
    return jnp.repeat(jnp.where(linked, 0.0, -1e30).astype(jnp.float32), BLOCK, axis=1)


def on_device(projected, upstream, w_out, partners):
    n, groups = lax.axis_size("seq"), lax.axis_size("dp")
    rows = projected.shape[1]
    factor = (rows * n * groups) ** (-0.5)
    bias = block_bias(partners, rows * n // BLOCK)
    grad, dw_t = layer(n, groups, factor, projected[0], upstream[0], bias, w_out)
    return grad[None], dw_t.T.astype(jnp.float32)


def solution(mesh):
    return jax.shard_map(
        on_device,
        mesh=mesh,
        in_specs=(P("dp", "seq", None), P("dp", "seq", None), P(), P()),
        out_specs=(P("dp", "seq", None), P(None, ("dp", "seq"))),
        check_vma=False,
    )
```

```python
import functools

import jax
import jax.numpy as jnp
from jax import lax
from jax.experimental import pallas as pl
from jax.experimental.pallas import tpu as pltpu
from jax.sharding import PartitionSpec as P

HD = 128
BLOCK = 128
PIECES = 4
MESH = pl.DeviceIdType.MESH
VMEM = pl.BlockSpec(memory_space=pltpu.VMEM)


def remote(src, dst, send_sem, recv_sem, **where):
    return pltpu.make_async_remote_copy(
        src_ref=src,
        dst_ref=dst,
        send_sem=send_sem,
        recv_sem=recv_sem,
        device_id=where,
        device_id_type=MESH,
    )


def greet(axes):
    barrier = pltpu.get_barrier_semaphore()
    count = 0
    for axis, size in axes:
        me = lax.axis_index(axis)
        for k in range(1, size):
            pl.semaphore_signal(
                barrier, inc=1, device_id={axis: lax.rem(me + k, size)}, device_id_type=MESH
            )
            count += 1
    pl.semaphore_wait(barrier, count)


def layer_kernel(
    n, groups, factor, proj_ref, up_ref, bias_ref, w_ref, grad_ref, out_ref, qkv, u_all, w_mine,
    og, kt, vt, dk_acc, dv_acc, dw_acc, grads, terms, held, total, q_send, q_recv, r_send, r_recv,
    l_send, l_recv, p_send, p_recv, g_send, g_recv, d_send, d_recv, w_send, w_recv, own_sem,
    own_q, own_g, own_w,
):
    me, mine = lax.axis_index("seq"), lax.axis_index("dp")
    rows = proj_ref.shape[0]
    width = proj_ref.shape[1] // 3
    length = n * rows
    heads = width // HD // n
    part = up_ref.shape[1] // groups
    columns = part // n
    chips = n // 2
    z = me // 2
    core = lax.rem(me, 2)
    partner = me + 1 - 2 * core
    scale = HD ** (-0.5)
    f32, bf16 = jnp.float32, jnp.bfloat16
    tile = min(2 * BLOCK, length)

    def dot(a, b, da, db):
        return lax.dot_general(a, b, (((da,), (db,)), ((), ())), preferred_element_type=f32)

    def span(index, size):
        return pl.ds(pl.multiple_of(index * size, size), size)

    size = rows // PIECES

    def u_rows(index, j):
        return u_all.at[pl.ds(pl.multiple_of(index * rows + j * size, size), size), :]

    def mine_rows(j):
        return up_ref.at[j * size : (j + 1) * size, :]

    def right(k, j, src):
        return remote(src, u_rows(me - 2 * k, j), r_send.at[k, j], r_recv.at[k, j], seq=me + 2)

    def left(k, j, src):
        return remote(src, u_rows(me + 2 * k, j), l_send.at[k, j], l_recv.at[k, j], seq=me - 2)

    def across(index, j, src):
        spot = index // 2
        return remote(src, u_rows(index, j), p_send.at[spot, j], p_recv.at[spot, j], seq=partner)

    def head_columns(t, device, h):
        return span(t * n * heads + device * heads + h, HD)

    def send_head(h):
        started = []
        for k in range(1, n):
            p = lax.rem(me + k, n)
            for t in range(3):
                copy = remote(
                    proj_ref.at[:, head_columns(t, p, h)],
                    qkv.at[h, t, span(me, rows), :],
                    q_send.at[h, t, k],
                    q_recv.at[h, t, k],
                    seq=p,
                )
                copy.start()
                started.append(copy)
        for t in range(3):
            copy = pltpu.make_async_copy(
                proj_ref.at[:, head_columns(t, me, h)],
                qkv.at[h, t, span(me, rows), :],
                own_q.at[h, t],
            )
            copy.start()
            started.append(copy)
        return started

    load_w = pltpu.make_async_copy(w_ref.at[span(me, heads * HD), :], w_mine, own_sem.at[0])
    load_w.start()
    greet((("seq", n), ("dp", groups)))

    for j in range(PIECES):

        @pl.when(z + 1 < chips)
        def _():
            right(0, j, mine_rows(j)).start()

        @pl.when(z >= 1)
        def _():
            left(0, j, mine_rows(j)).start()

    for j in range(PIECES):
        across(me, j, mine_rows(j)).start()
    own_u = pltpu.make_async_copy(up_ref, u_all.at[span(me, rows), :], own_sem.at[1])
    own_u.start()
    arriving = []
    for k in range(1, chips):
        while len(arriving) < min(heads, k - 1):
            arriving.append(send_head(len(arriving)))
        for j in range(PIECES):

            @pl.when(z - k >= 0)
            def _():
                right(k - 1, j, mine_rows(j)).wait_recv()
                block = me - 2 * k

                @pl.when(z + 1 < chips)
                def _():
                    right(k, j, u_rows(block, j)).start()

                across(block, j, u_rows(block, j)).start()

            @pl.when(z + k < chips)
            def _():
                left(k - 1, j, mine_rows(j)).wait_recv()
                block = me + 2 * k

                @pl.when(z >= 1)
                def _():
                    left(k, j, u_rows(block, j)).start()

                across(block, j, u_rows(block, j)).start()

    while len(arriving) < heads:
        arriving.append(send_head(len(arriving)))
    load_w.wait()
    own_u.wait()
    for i in range(chips):
        for j in range(PIECES):
            across(2 * i + core, j, mine_rows(j)).wait_recv()

    def out_grad_step(i, carry):
        u = u_all[span(i, tile), :]
        og[:, span(i, tile)] = dot(w_mine[...], u, 1, 1).astype(bf16)
        return carry

    lax.fori_loop(0, length // tile, out_grad_step, 0)
    leaving = []
    sums = []
    for h in range(heads):
        for copy in arriving[h]:
            copy.wait()
        kt[...] = qkv[h, 1].astype(f32).T.astype(bf16)
        vt[...] = qkv[h, 2].astype(f32).T.astype(bf16)
        dk_acc[...] = jnp.zeros_like(dk_acc)
        dv_acc[...] = jnp.zeros_like(dv_acc)
        dw_acc[...] = jnp.zeros_like(dw_acc)

        def tile_step(i, carry):
            at = span(i, tile)
            q, k, v = qkv[h, 0, at, :], qkv[h, 1], qkv[h, 2]
            grad_t = og[h * HD : (h + 1) * HD, at]
            grad_t32 = grad_t.astype(f32)
            scores = dot(k, q, 1, 1) * scale
            scores = scores.reshape(length // BLOCK, BLOCK, tile) + bias_ref[:, at][:, None, :]
            scores = scores.reshape(length, tile)
            exponent = jnp.exp(scores - jnp.max(scores, axis=0, keepdims=True))
            inverse = 1.0 / jnp.sum(exponent, axis=0, keepdims=True)
            att = dot(vt[...], exponent.astype(bf16), 1, 0) * inverse
            delta = jnp.sum(grad_t32 * att, axis=0, keepdims=True)
            probs = exponent * inverse
            score_grad = (probs * (dot(v, grad_t, 1, 0) - delta)).astype(bf16)
            grads[h, 0, at, :] = (dot(kt[...], score_grad, 1, 0) * scale).T.astype(bf16)
            dk_acc[...] += dot(score_grad, q, 1, 0)
            dv_acc[...] += dot(probs.astype(bf16), grad_t32.T.astype(bf16), 1, 0)
            dw_acc[...] += dot(att.astype(bf16), u_all[at, :], 1, 0)
            return carry

        lax.fori_loop(0, length // tile, tile_step, 0)
        terms[h] = (dw_acc[...] * factor).astype(bf16)
        for k in range(1, groups):
            p = lax.rem(mine + k, groups)
            copy = remote(
                terms.at[h, :, span(p, part)],
                held.at[h, k - 1],
                d_send.at[h, k],
                d_recv.at[h, k],
                dp=p,
            )
            copy.start()
            sums.append(copy)
        grads[h, 1] = (dk_acc[...] * scale).astype(bf16)
        grads[h, 2] = dv_acc[...].astype(bf16)
        for k in range(1, n):
            p = lax.rem(me + k, n)
            for t in range(3):
                copy = remote(
                    grads.at[h, t, span(p, rows), :],
                    grad_ref.at[:, head_columns(t, me, h)],
                    g_send.at[h, t, k],
                    g_recv.at[h, t, k],
                    seq=p,
                )
                copy.start()
                leaving.append(copy)
        for t in range(3):
            copy = pltpu.make_async_copy(
                grads.at[h, t, span(me, rows), :],
                grad_ref.at[:, head_columns(t, me, h)],
                own_g.at[h, t],
            )
            copy.start()
            leaving.append(copy)
    for copy in sums:
        copy.wait()
    for h in range(heads):
        summed = terms[h, :, span(mine, part)].astype(f32)
        for k in range(groups - 1):
            summed = summed + held[h, k].astype(f32)
        total[h] = summed.T.astype(bf16)
        spot = out_ref.at[:, span(me * heads + h, HD)]
        for k in range(1, n):
            p = lax.rem(me + k, n)
            copy = remote(
                total.at[h, span(p, columns), :], spot, w_send.at[h, k], w_recv.at[h, k], seq=p
            )
            copy.start()
            leaving.append(copy)
        copy = pltpu.make_async_copy(total.at[h, span(me, columns), :], spot, own_w.at[h])
        copy.start()
        leaving.append(copy)
    for copy in leaving:
        copy.wait()
    for j in range(PIECES):
        for i in range(chips):
            across(2 * i + core, j, mine_rows(j)).wait_send()
        for k in range(chips):

            @pl.when((z - k >= 0) & (z + 1 < chips))
            def _():
                right(k, j, mine_rows(j)).wait_send()

            @pl.when((z + k < chips) & (z >= 1))
            def _():
                left(k, j, mine_rows(j)).wait_send()


def layer(n, groups, factor, proj, up, bias, w_out):
    rows, width3 = proj.shape
    width = width3 // 3
    heads = width // HD // n
    length, depth = n * rows, up.shape[1]
    part = depth // groups
    chips = n // 2
    f32, bf16 = jnp.float32, jnp.bfloat16
    dma = pltpu.SemaphoreType.DMA
    return pl.pallas_call(
        functools.partial(layer_kernel, n, groups, factor),
        out_shape=(
            jax.ShapeDtypeStruct((rows, width3), bf16),
            jax.ShapeDtypeStruct((part // n, width), bf16),
        ),
        in_specs=[VMEM] * 3 + [pl.BlockSpec(memory_space=pl.ANY)],
        out_specs=(VMEM, VMEM),
        scratch_shapes=[
            pltpu.VMEM((heads, 3, length, HD), bf16),
            pltpu.VMEM((length, depth), bf16),
            pltpu.VMEM((heads * HD, depth), bf16),
            pltpu.VMEM((heads * HD, length), bf16),
            pltpu.VMEM((HD, length), bf16),
            pltpu.VMEM((HD, length), bf16),
            pltpu.VMEM((length, HD), f32),
            pltpu.VMEM((length, HD), f32),
            pltpu.VMEM((HD, depth), f32),
            pltpu.VMEM((heads, 3, length, HD), bf16),
            pltpu.VMEM((heads, HD, depth), bf16),
            pltpu.VMEM((heads, max(groups - 1, 1), HD, part), bf16),
            pltpu.VMEM((heads, part, HD), bf16),
            dma((heads, 3, n)),
            dma((heads, 3, n)),
        ]
        + [dma((chips, PIECES))] * 6
        + [
            dma((heads, 3, n)),
            dma((heads, 3, n)),
            dma((heads, groups)),
            dma((heads, groups)),
            dma((heads, n)),
            dma((heads, n)),
            dma((2,)),
            dma((heads, 3)),
            dma((heads, 3)),
            dma((heads,)),
        ],
        compiler_params=pltpu.CompilerParams(
            collective_id=0, has_side_effects=True, vmem_limit_bytes=60 * 2**20
        ),
        name="layer",
    )(proj, up, bias, w_out)


def block_bias(partners, total):
    ids = jnp.arange(total, dtype=jnp.int32)
    chosen = jnp.any(partners[:, :, None] == ids[None, None, :], axis=1)
    near = jnp.abs(ids[:, None] - ids[None, :]) <= 1
    border = (ids == 0) | (ids == total - 1)
    linked = chosen | chosen.T | near | border[:, None] | border[None, :]
    return jnp.repeat(jnp.where(linked, 0.0, -1e30).astype(jnp.float32), BLOCK, axis=1)


def on_device(projected, upstream, w_out, partners):
    n, groups = lax.axis_size("seq"), lax.axis_size("dp")
    rows = projected.shape[1]
    factor = (rows * n * groups) ** (-0.5)
    bias = block_bias(partners, rows * n // BLOCK)
    grad, dw_t = layer(n, groups, factor, projected[0], upstream[0], bias, w_out)
    return grad[None], dw_t.T.astype(jnp.float32)


def solution(mesh):
    return jax.shard_map(
        on_device,
        mesh=mesh,
        in_specs=(P("dp", "seq", None), P("dp", "seq", None), P(), P()),
        out_specs=(P("dp", "seq", None), P(None, ("dp", "seq"))),
        check_vma=False,
    )
```

```python
import functools

import jax
import jax.numpy as jnp
from jax import lax
from jax.experimental import pallas as pl
from jax.experimental.pallas import tpu as pltpu
from jax.sharding import PartitionSpec as P

HD = 128
BLOCK = 128
PIECES = 4
MESH = pl.DeviceIdType.MESH
VMEM = pl.BlockSpec(memory_space=pltpu.VMEM)


def remote(src, dst, send_sem, recv_sem, **where):
    return pltpu.make_async_remote_copy(
        src_ref=src,
        dst_ref=dst,
        send_sem=send_sem,
        recv_sem=recv_sem,
        device_id=where,
        device_id_type=MESH,
    )


def greet(axes):
    barrier = pltpu.get_barrier_semaphore()
    count = 0
    for axis, size in axes:
        me = lax.axis_index(axis)
        for k in range(1, size):
            pl.semaphore_signal(
                barrier, inc=1, device_id={axis: lax.rem(me + k, size)}, device_id_type=MESH
            )
            count += 1
    pl.semaphore_wait(barrier, count)


def layer_kernel(
    n, groups, factor, proj_ref, up_ref, bias_ref, w_ref, grad_ref, out_ref, qkv, u_all, w_mine,
    og, kt, vt, dk_acc, dv_acc, dw_acc, grads, terms, held, total, q_send, q_recv, r_send, r_recv,
    l_send, l_recv, p_send, p_recv, g_send, g_recv, d_send, d_recv, w_send, w_recv, own_sem,
    own_q, own_g, own_w,
):
    me, mine = lax.axis_index("seq"), lax.axis_index("dp")
    rows = proj_ref.shape[0]
    width = proj_ref.shape[1] // 3
    length = n * rows
    heads = width // HD // n
    part = up_ref.shape[1] // groups
    columns = part // n
    chips = n // 2
    z = me // 2
    core = lax.rem(me, 2)
    partner = me + 1 - 2 * core
    scale = HD ** (-0.5)
    f32, bf16 = jnp.float32, jnp.bfloat16
    tile = min(2 * BLOCK, length)

    def dot(a, b, da, db):
        return lax.dot_general(a, b, (((da,), (db,)), ((), ())), preferred_element_type=f32)

    def span(index, size):
        return pl.ds(pl.multiple_of(index * size, size), size)

    size = rows // PIECES

    def u_rows(index, j):
        return u_all.at[pl.ds(pl.multiple_of(index * rows + j * size, size), size), :]

    def mine_rows(j):
        return up_ref.at[j * size : (j + 1) * size, :]

    def right(k, j, src):
        return remote(src, u_rows(me - 2 * k, j), r_send.at[k, j], r_recv.at[k, j], seq=me + 2)

    def left(k, j, src):
        return remote(src, u_rows(me + 2 * k, j), l_send.at[k, j], l_recv.at[k, j], seq=me - 2)

    def across(index, j, src):
        spot = index // 2
        return remote(src, u_rows(index, j), p_send.at[spot, j], p_recv.at[spot, j], seq=partner)

    def head_columns(t, device, h):
        return span(t * n * heads + device * heads + h, HD)

    def send_head(h):
        started = []
        for k in range(1, n):
            p = lax.rem(me + k, n)
            for t in range(3):
                copy = remote(
                    proj_ref.at[:, head_columns(t, p, h)],
                    qkv.at[h, t, span(me, rows), :],
                    q_send.at[h, t, k],
                    q_recv.at[h, t, k],
                    seq=p,
                )
                copy.start()
                started.append(copy)
        for t in range(3):
            copy = pltpu.make_async_copy(
                proj_ref.at[:, head_columns(t, me, h)],
                qkv.at[h, t, span(me, rows), :],
                own_q.at[h, t],
            )
            copy.start()
            started.append(copy)
        return started

    load_w = pltpu.make_async_copy(w_ref.at[span(me, heads * HD), :], w_mine, own_sem.at[0])
    load_w.start()
    greet((("seq", n), ("dp", groups)))

    for j in range(PIECES):

        @pl.when(z + 1 < chips)
        def _():
            right(0, j, mine_rows(j)).start()

        @pl.when(z >= 1)
        def _():
            left(0, j, mine_rows(j)).start()

    for j in range(PIECES):
        across(me, j, mine_rows(j)).start()
    own_u = pltpu.make_async_copy(up_ref, u_all.at[span(me, rows), :], own_sem.at[1])
    own_u.start()
    arriving = []
    for k in range(1, chips):
        while len(arriving) < min(heads, k - 1):
            arriving.append(send_head(len(arriving)))
        for j in range(PIECES):

            @pl.when(z - k >= 0)
            def _():
                right(k - 1, j, mine_rows(j)).wait_recv()
                block = me - 2 * k

                @pl.when(z + 1 < chips)
                def _():
                    right(k, j, u_rows(block, j)).start()

                across(block, j, u_rows(block, j)).start()

            @pl.when(z + k < chips)
            def _():
                left(k - 1, j, mine_rows(j)).wait_recv()
                block = me + 2 * k

                @pl.when(z >= 1)
                def _():
                    left(k, j, u_rows(block, j)).start()

                across(block, j, u_rows(block, j)).start()

    while len(arriving) < heads:
        arriving.append(send_head(len(arriving)))
    load_w.wait()
    own_u.wait()
    for i in range(chips):
        for j in range(PIECES):
            across(2 * i + core, j, mine_rows(j)).wait_recv()

    def out_grad_step(i, carry):
        u = u_all[span(i, tile), :]
        og[:, span(i, tile)] = dot(w_mine[...], u, 1, 1).astype(bf16)
        return carry

    lax.fori_loop(0, length // tile, out_grad_step, 0)
    leaving = []
    sums = []

    def finish(h):
        for copy in sums[h]:
            copy.wait()
        summed = terms[h, :, span(mine, part)].astype(f32)
        for k in range(groups - 1):
            summed = summed + held[h, k].astype(f32)
        total[h] = summed.T.astype(bf16)
        spot = out_ref.at[:, span(me * heads + h, HD)]
        for k in range(1, n):
            p = lax.rem(me + k, n)
            copy = remote(
                total.at[h, span(p, columns), :], spot, w_send.at[h, k], w_recv.at[h, k], seq=p
            )
            copy.start()
            leaving.append(copy)
        copy = pltpu.make_async_copy(total.at[h, span(me, columns), :], spot, own_w.at[h])
        copy.start()
        leaving.append(copy)

    for h in range(heads):
        for copy in arriving[h]:
            copy.wait()
        kt[...] = qkv[h, 1].astype(f32).T.astype(bf16)
        vt[...] = qkv[h, 2].astype(f32).T.astype(bf16)
        dk_acc[...] = jnp.zeros_like(dk_acc)
        dv_acc[...] = jnp.zeros_like(dv_acc)
        dw_acc[...] = jnp.zeros_like(dw_acc)

        def tile_step(i, carry):
            at = span(i, tile)
            q, k, v = qkv[h, 0, at, :], qkv[h, 1], qkv[h, 2]
            grad_t = og[h * HD : (h + 1) * HD, at]
            grad_t32 = grad_t.astype(f32)
            scores = dot(k, q, 1, 1) * scale
            scores = scores.reshape(length // BLOCK, BLOCK, tile) + bias_ref[:, at][:, None, :]
            scores = scores.reshape(length, tile)
            exponent = jnp.exp(scores - jnp.max(scores, axis=0, keepdims=True))
            inverse = 1.0 / jnp.sum(exponent, axis=0, keepdims=True)
            att = dot(vt[...], exponent.astype(bf16), 1, 0) * inverse
            delta = jnp.sum(grad_t32 * att, axis=0, keepdims=True)
            probs = exponent * inverse
            score_grad = (probs * (dot(v, grad_t, 1, 0) - delta)).astype(bf16)
            grads[h, 0, at, :] = (dot(kt[...], score_grad, 1, 0) * scale).T.astype(bf16)
            dk_acc[...] += dot(score_grad, q, 1, 0)
            dv_acc[...] += dot(probs.astype(bf16), grad_t32.T.astype(bf16), 1, 0)
            dw_acc[...] += dot(att.astype(bf16), u_all[at, :], 1, 0)
            return carry

        lax.fori_loop(0, length // tile, tile_step, 0)
        sums.append([])
        terms[h] = (dw_acc[...] * factor).astype(bf16)
        for k in range(1, groups):
            p = lax.rem(mine + k, groups)
            copy = remote(
                terms.at[h, :, span(p, part)],
                held.at[h, k - 1],
                d_send.at[h, k],
                d_recv.at[h, k],
                dp=p,
            )
            copy.start()
            sums[h].append(copy)
        if h > 0:
            finish(h - 1)
        grads[h, 1] = (dk_acc[...] * scale).astype(bf16)
        grads[h, 2] = dv_acc[...].astype(bf16)
        for k in range(1, n):
            p = lax.rem(me + k, n)
            for t in range(3):
                copy = remote(
                    grads.at[h, t, span(p, rows), :],
                    grad_ref.at[:, head_columns(t, me, h)],
                    g_send.at[h, t, k],
                    g_recv.at[h, t, k],
                    seq=p,
                )
                copy.start()
                leaving.append(copy)
        for t in range(3):
            copy = pltpu.make_async_copy(
                grads.at[h, t, span(me, rows), :],
                grad_ref.at[:, head_columns(t, me, h)],
                own_g.at[h, t],
            )
            copy.start()
            leaving.append(copy)
    finish(heads - 1)
    for copy in leaving:
        copy.wait()
    for j in range(PIECES):
        for i in range(chips):
            across(2 * i + core, j, mine_rows(j)).wait_send()
        for k in range(chips):

            @pl.when((z - k >= 0) & (z + 1 < chips))
            def _():
                right(k, j, mine_rows(j)).wait_send()

            @pl.when((z + k < chips) & (z >= 1))
            def _():
                left(k, j, mine_rows(j)).wait_send()


def layer(n, groups, factor, proj, up, bias, w_out):
    rows, width3 = proj.shape
    width = width3 // 3
    heads = width // HD // n
    length, depth = n * rows, up.shape[1]
    part = depth // groups
    chips = n // 2
    f32, bf16 = jnp.float32, jnp.bfloat16
    dma = pltpu.SemaphoreType.DMA
    return pl.pallas_call(
        functools.partial(layer_kernel, n, groups, factor),
        out_shape=(
            jax.ShapeDtypeStruct((rows, width3), bf16),
            jax.ShapeDtypeStruct((part // n, width), bf16),
        ),
        in_specs=[VMEM] * 3 + [pl.BlockSpec(memory_space=pl.ANY)],
        out_specs=(VMEM, VMEM),
        scratch_shapes=[
            pltpu.VMEM((heads, 3, length, HD), bf16),
            pltpu.VMEM((length, depth), bf16),
            pltpu.VMEM((heads * HD, depth), bf16),
            pltpu.VMEM((heads * HD, length), bf16),
            pltpu.VMEM((HD, length), bf16),
            pltpu.VMEM((HD, length), bf16),
            pltpu.VMEM((length, HD), f32),
            pltpu.VMEM((length, HD), f32),
            pltpu.VMEM((HD, depth), f32),
            pltpu.VMEM((heads, 3, length, HD), bf16),
            pltpu.VMEM((heads, HD, depth), bf16),
            pltpu.VMEM((heads, max(groups - 1, 1), HD, part), bf16),
            pltpu.VMEM((heads, part, HD), bf16),
            dma((heads, 3, n)),
            dma((heads, 3, n)),
        ]
        + [dma((chips, PIECES))] * 6
        + [
            dma((heads, 3, n)),
            dma((heads, 3, n)),
            dma((heads, groups)),
            dma((heads, groups)),
            dma((heads, n)),
            dma((heads, n)),
            dma((2,)),
            dma((heads, 3)),
            dma((heads, 3)),
            dma((heads,)),
        ],
        compiler_params=pltpu.CompilerParams(
            collective_id=0, has_side_effects=True, vmem_limit_bytes=60 * 2**20
        ),
        name="layer",
    )(proj, up, bias, w_out)


def block_bias(partners, total):
    ids = jnp.arange(total, dtype=jnp.int32)
    chosen = jnp.any(partners[:, :, None] == ids[None, None, :], axis=1)
    near = jnp.abs(ids[:, None] - ids[None, :]) <= 1
    border = (ids == 0) | (ids == total - 1)
    linked = chosen | chosen.T | near | border[:, None] | border[None, :]
    return jnp.repeat(jnp.where(linked, 0.0, -1e30).astype(jnp.float32), BLOCK, axis=1)


def on_device(projected, upstream, w_out, partners):
    n, groups = lax.axis_size("seq"), lax.axis_size("dp")
    rows = projected.shape[1]
    factor = (rows * n * groups) ** (-0.5)
    bias = block_bias(partners, rows * n // BLOCK)
    grad, dw_t = layer(n, groups, factor, projected[0], upstream[0], bias, w_out)
    return grad[None], dw_t.T.astype(jnp.float32)


def solution(mesh):
    return jax.shard_map(
        on_device,
        mesh=mesh,
        in_specs=(P("dp", "seq", None), P("dp", "seq", None), P(), P()),
        out_specs=(P("dp", "seq", None), P(None, ("dp", "seq"))),
        check_vma=False,
    )
```
